32 devices in a mesh: dp: 8 (over y, x, core), seq: 4 (over z).
Axes of the slice: x: 2, y: 2, z: 4, core: 2. Of those that a mesh axis runs over, the one named last changes fastest.
Arguments:
- tokens: bfloat16 [8, 2048, 768], P('dp', 'seq'), may hold values from -6 to 6
- cotangent: bfloat16 [8, 2048, 768], P('dp', 'seq'), may hold values from -6 to 6
- w_query: bfloat16 [768, 768], P(('dp', 'seq')), may hold values from -0.21875 to 0.21875
- w_key: bfloat16 [768, 768], P(('dp', 'seq')), may hold values from -0.21875 to 0.21875
- w_value: bfloat16 [768, 768], P(('dp', 'seq')), may hold values from -0.375 to 0.375
- w_output: bfloat16 [768, 768], P(('dp', 'seq')), may hold values from -0.375 to 0.375
- w_inner: bfloat16 [768, 3072], P(('dp', 'seq')), may hold values from -0.375 to 0.375
- w_outer: bfloat16 [3072, 768], P(('dp', 'seq')), may hold values from -0.1875 to 0.1875
- bias_query: bfloat16 [768], P(('dp', 'seq')), may hold values from -1.5 to 1.5
- bias_value: bfloat16 [768], P(('dp', 'seq')), may hold values from -1.5 to 1.5
- bias_output: bfloat16 [768], P(('dp', 'seq')), may hold values from -1.5 to 1.5
- bias_inner: bfloat16 [3072], P(('dp', 'seq')), may hold values from -1.5 to 1.5
- bias_outer: bfloat16 [768], P(('dp', 'seq')), may hold values from -1.5 to 1.5
- gain_input: bfloat16 [768], P(('dp', 'seq')), may hold values from 0.25 to 1.75
- bias_input: bfloat16 [768], P(('dp', 'seq')), may hold values from -1.5 to 1.5
- gain_attend: bfloat16 [768], P(('dp', 'seq')), may hold values from 0.25 to 1.75
- bias_attend: bfloat16 [768], P(('dp', 'seq')), may hold values from -1.5 to 1.5
- gain_middle: bfloat16 [768], P(('dp', 'seq')), may hold values from 0.25 to 1.75
- bias_middle: bfloat16 [768], P(('dp', 'seq')), may hold values from -1.5 to 1.5
- gain_hidden: bfloat16 [3072], P(('dp', 'seq')), may hold values from 0.25 to 1.75
- bias_hidden: bfloat16 [3072], P(('dp', 'seq')), may hold values from -1.5 to 1.5
Outputs:
- output: bfloat16 [8, 2048, 768], P('dp', 'seq')
- grad_tokens: float32 [8, 2048, 768], P('dp', 'seq')
- grad_w_query: float32 [768, 768], P(('dp', 'seq'))
- grad_w_key: float32 [768, 768], P(('dp', 'seq'))
- grad_w_value: float32 [768, 768], P(('dp', 'seq'))
- grad_w_output: float32 [768, 768], P(('dp', 'seq'))
- grad_w_inner: float32 [768, 3072], P(('dp', 'seq'))
- grad_w_outer: float32 [3072, 768], P(('dp', 'seq'))
- grad_bias_query: float32 [768], P(('dp', 'seq'))
- grad_bias_value: float32 [768], P(('dp', 'seq'))
- grad_bias_output: float32 [768], P(('dp', 'seq'))
- grad_bias_inner: float32 [3072], P(('dp', 'seq'))
- grad_bias_outer: float32 [768], P(('dp', 'seq'))
- grad_gain_input: float32 [768], P(('dp', 'seq'))
- grad_bias_input: float32 [768], P(('dp', 'seq'))
- grad_gain_attend: float32 [768], P(('dp', 'seq'))
- grad_bias_attend: float32 [768], P(('dp', 'seq'))
- grad_gain_middle: float32 [768], P(('dp', 'seq'))
- grad_bias_middle: float32 [768], P(('dp', 'seq'))
- grad_gain_hidden: float32 [3072], P(('dp', 'seq'))
- grad_bias_hidden: float32 [3072], P(('dp', 'seq'))
The draws below stay inside these ranges and needn't reach their ends.
All inputs are finite; a program needn't handle non-finite values.
Results may differ from the reference program's by a relative error of at most 0.02.
Values may be sent and summed in bfloat16 or wider, within the bound.
No kernel may reach another device: no remote copies, remote signals or barrier semaphores. Data moves between devices by JAX's collectives and lax.ppermute only.
A program may use at most 192 MiB of HBM per device.

```python
import jax
import jax.numpy as jnp
from jax import lax

D = 768
HEADS = 12
HEAD = 64
FF = 3072
SEQ_LEN = 2048
BLOCK = 256
SEQS = 8


def spiked(result, rng, source, target, blocks, factor):
    def block_of(position):
        return (jnp.arange(result.shape[position]) // (result.shape[position] // blocks)).reshape((-1,) + (1,) * (result.ndim - 1 - position))

    one_side = jax.random.permutation(rng, blocks)[block_of(target)]
    other_side = (block_of(target) + blocks // 2) % blocks
    return jnp.where((block_of(source) == one_side) | (block_of(source) == other_side), factor * result, result)


def levels(rng, shape, cuts, least, high):
    def one(axis_at, shards_of):
        heights = jax.random.uniform(jax.random.fold_in(jax.random.fold_in(rng, 6), axis_at), (shards_of,), jnp.float32, least / len(cuts), high / len(cuts))
        return jnp.repeat(jnp.exp(heights), shape[axis_at] // shards_of).reshape((-1,) + (1,) * (len(shape) - axis_at - 1))

    loudness = one(*cuts[0])
    for cut in cuts[1:]:
        loudness = loudness * one(*cut)
    return loudness


def gaussian(rng, shape, spread, bound, split=(), kind=jnp.bfloat16):
    result = jax.random.normal(rng, shape, jnp.float32) * spread
    if len(split) > 0:
        result = levels(rng, shape, split, -0.22, 0.18) * result
    return jnp.clip(result, min=-bound, max=bound).astype(kind)


def gaussian_with(stream_key, shape, width, bound, shards, heavy, held_as=jnp.bfloat16):
    drawn = width * jax.random.normal(stream_key, shape, jnp.float32)
    if shards:
        drawn = drawn * levels(stream_key, shape, shards, -0.22, 0.18)
    return jnp.clip(spiked(drawn, jax.random.fold_in(stream_key, 3), *heavy), -bound, bound).astype(held_as)


def setup_inputs(seed: int = 0) -> dict:
    splits = jax.random.split(jax.random.key(seed), 22)
    tokens = gaussian_with(splits[0], (SEQS, SEQ_LEN, D), 1.0, 6.0, ((0, 8), (1, 4)), (0, 2, 8, 2.0))
    cotangent = gaussian(splits[1], (SEQS, SEQ_LEN, D), 1.0, 6.0, ((0, 8), (1, 4)))
    w_query = gaussian(splits[2], (D, D), D ** -0.5, 0.21875, ((0, 32),))
    w_key = gaussian(splits[3], (D, D), D ** -0.5, 0.21875, ((0, 32),))
    w_value = gaussian(splits[4], (D, D), (D * 1000 // 3178) ** -0.5, 0.375, ((0, 32),))
    w_output = gaussian(splits[5], (D, D), (D * 1000 // 3178) ** -0.5, 0.375, ((0, 32),))
    w_inner = gaussian(splits[6], (D, FF), (D * 1000 // 3178) ** -0.5, 0.375, ((0, 32),))
    w_outer = gaussian(splits[7], (FF, D), (FF * 1000 // 3178) ** -0.5, 0.1875, ((0, 32),))
    bias_query = gaussian(splits[8], (D,), 0.3, 1.5, ((0, 32),))
    bias_value = gaussian(splits[9], (D,), 0.3, 1.5, ((0, 32),))
    bias_output = gaussian(splits[10], (D,), 0.3, 1.5, ((0, 32),))
    bias_inner = gaussian(splits[11], (FF,), 0.3, 1.5, ((0, 32),))
    bias_outer = gaussian(splits[12], (D,), 0.3, 1.5, ((0, 32),))
    gain_input = jnp.clip(1.0 + 0.15 * jax.random.normal(splits[13], (D,), jnp.float32), 0.25, 1.75).astype(jnp.bfloat16)
    bias_input = gaussian(splits[14], (D,), 0.3, 1.5, ((0, 32),))
    gain_attend = jnp.clip(1.0 + 0.15 * jax.random.normal(splits[15], (D,), jnp.float32), 0.25, 1.75).astype(jnp.bfloat16)
    bias_attend = gaussian(splits[16], (D,), 0.3, 1.5, ((0, 32),))
    gain_middle = jnp.clip(1.0 + 0.15 * jax.random.normal(splits[17], (D,), jnp.float32), 0.25, 1.75).astype(jnp.bfloat16)
    bias_middle = gaussian(splits[18], (D,), 0.3, 1.5, ((0, 32),))
    gain_hidden = jnp.clip(1.0 + 0.15 * jax.random.normal(splits[19], (FF,), jnp.float32), 0.25, 1.75).astype(jnp.bfloat16)
    bias_hidden = gaussian(splits[20], (FF,), 0.3, 1.5, ((0, 32),))
    return dict(tokens=tokens, cotangent=cotangent, w_query=w_query, w_key=w_key, w_value=w_value, w_output=w_output, w_inner=w_inner, w_outer=w_outer, bias_query=bias_query, bias_value=bias_value, bias_output=bias_output, bias_inner=bias_inner, bias_outer=bias_outer, gain_input=gain_input, bias_input=bias_input, gain_attend=gain_attend, bias_attend=bias_attend, gain_middle=gain_middle, bias_middle=bias_middle, gain_hidden=gain_hidden, bias_hidden=bias_hidden)


@jax.custom_vjp
def low(v):
    return lax.optimization_barrier(v.astype(jnp.bfloat16)).astype(jnp.float32)

@jax.custom_vjp
def low_back(v):
    return v

def low_keep(v):
    return (low(v), None)

def low_pass(kept, grad):
    return (grad,)

def back_keep(v):
    return (v, None)

def back_low(kept, grad):
    return (low(grad),)
low.defvjp(low_keep, low_pass)
low_back.defvjp(back_keep, back_low)
EPSILON = 1e-05
MASKED = -1e+30

def layer_norm(values, scaling, offset):
    centered = values - lax.optimization_barrier(jnp.mean(values, axis=-1, keepdims=True))
    variance = lax.optimization_barrier(jnp.mean(centered * centered, axis=-1, keepdims=True))
    return centered * lax.rsqrt(variance + EPSILON) * scaling + offset

def matmul(former, latter):
    return jnp.dot(former, latter, precision=lax.Precision.HIGHEST)

def attend_rows(query_rows, keys_all, values_all, first_row):
    count = query_rows.shape[0]
    query_pos = first_row + jnp.arange(count, dtype=jnp.int32)
    key_pos = jnp.arange(keys_all.shape[0], dtype=jnp.int32)
    visible = key_pos[None, :] // BLOCK <= query_pos[:, None] // BLOCK
    scores = jnp.einsum('qhd,khd->hqk', query_rows, keys_all, precision=lax.Precision.HIGHEST) * HEAD ** (-0.5)
    scores = low_back(scores)
    masked = jnp.where(visible[None, :, :], scores, MASKED)
    largest = lax.optimization_barrier(jnp.max(masked, axis=-1, keepdims=True))
    powered = jnp.exp(masked - largest)
    shares = low(powered / lax.optimization_barrier(jnp.sum(powered, axis=-1, keepdims=True)))
    return jnp.einsum('hqk,khd->qhd', shares, values_all, precision=lax.Precision.HIGHEST)

def forward(sequence, params):
    w_query, w_key, w_value, w_output, w_inner, w_outer, bias_query, bias_value, bias_output, bias_inner, bias_outer, gain_input, bias_input, gain_attend, bias_attend, gain_middle, bias_middle, gain_hidden, bias_hidden = params
    normed = low(layer_norm(sequence, gain_input, bias_input))
    queries = low(low_back(matmul(normed, w_query) + bias_query))
    keys_all = low(low_back(matmul(normed, w_key)))
    values_all = low(low_back(matmul(normed, w_value) + bias_value))
    block_rows = min(512, SEQ_LEN)
    count = SEQ_LEN // block_rows
    query_blocks = queries.reshape(count, block_rows, HEADS, HEAD)
    starts = jnp.arange(count, dtype=jnp.int32) * block_rows
    keys_heads = keys_all.reshape(SEQ_LEN, HEADS, HEAD)
    values_heads = values_all.reshape(SEQ_LEN, HEADS, HEAD)
    checked = jax.checkpoint(attend_rows)
    attended = lax.map(lambda pair: checked(pair[0], keys_heads, values_heads, pair[1]), (query_blocks, starts))
    attended = low_back(attended.reshape(SEQ_LEN, D))
    sub_normed = low(layer_norm(attended, gain_attend, bias_attend))
    branch = low_back(matmul(sub_normed, w_output) + bias_output)
    middle = sequence + branch
    normed_mid = low(layer_norm(middle, gain_middle, bias_middle))
    hidden_pre = low_back(matmul(normed_mid, w_inner) + bias_inner)
    hidden_low = low(layer_norm(jax.nn.gelu(hidden_pre, approximate=False), gain_hidden, bias_hidden))
    ffn_out = low_back(matmul(hidden_low, w_outer) + bias_outer)
    return middle + ffn_out

def reference(tokens, cotangent, w_query, w_key, w_value, w_output, w_inner, w_outer, bias_query, bias_value, bias_output, bias_inner, bias_outer, gain_input, bias_input, gain_attend, bias_attend, gain_middle, bias_middle, gain_hidden, bias_hidden):
    params = (w_query, w_key, w_value, w_output, w_inner, w_outer, bias_query, bias_value, bias_output, bias_inner, bias_outer, gain_input, bias_input, gain_attend, bias_attend, gain_middle, bias_middle, gain_hidden, bias_hidden)
    params = tuple((member.astype(jnp.float32) for member in params))
    sequences = tokens.astype(jnp.float32)
    cotangents = cotangent.astype(jnp.float32)

    def one_sequence(totals, pair):
        outputs, pull = jax.vjp(forward, pair[0], params)
        grad_sequence, grad_params = pull(pair[1])
        totals = tuple((total + grad for total, grad in zip(totals, grad_params)))
        return (totals, (outputs.astype(jnp.bfloat16), grad_sequence))
    zeros = tuple((jnp.zeros_like(member) for member in params))
    totals, (outputs, grads) = lax.scan(one_sequence, zeros, (sequences, cotangents))
    return (outputs, grads, totals[0], totals[1], totals[2], totals[3], totals[4], totals[5], totals[6], totals[7], totals[8], totals[9], totals[10], totals[11], totals[12], totals[13], totals[14], totals[15], totals[16], totals[17], totals[18])
```

```python
import jax
import jax.numpy as jnp
from jax import lax
from jax.experimental import pallas as pl
from jax.experimental.pallas import tpu as pltpu
from jax.sharding import PartitionSpec as P


HEAD = 64
BLOCK = 256


EPSILON = 1e-05
MASKED = -1e30


def layer_norm(values, scaling, offset):
    centered = values - jnp.mean(values, axis=-1, keepdims=True)
    variance = jnp.mean(centered * centered, axis=-1, keepdims=True)
    return centered * lax.rsqrt(variance + EPSILON) * scaling + offset


def hidden_norm(hidden_pre, scaling, offset):
    return layer_norm(jax.nn.gelu(hidden_pre, approximate=False), scaling, offset)


def product(former, latter):
    return jnp.dot(former, latter, preferred_element_type=jnp.float32)


def product_left(former, latter):
    return jnp.einsum("ta,tb->ab", former, latter, preferred_element_type=jnp.float32)


def product_right(former, latter):
    return jnp.einsum("ta,ba->tb", former, latter, preferred_element_type=jnp.float32)


def column_sums(matrix):
    return jnp.sum(matrix.astype(jnp.float32), axis=0)


def head_pair(matrix, head_turn):
    pair_width = 2 * HEAD
    columns = lax.dynamic_slice_in_dim(matrix, head_turn * pair_width, pair_width, 2)
    return columns.reshape(matrix.shape[0], matrix.shape[1], 2, HEAD)


def place_pair(whole, part, head_turn):
    pair_width = 2 * HEAD
    flat_part = part.reshape(whole.shape[0], whole.shape[1], pair_width)
    return lax.dynamic_update_slice_in_dim(whole, flat_part, head_turn * pair_width, 2)


def stat_pair(stats, head_turn):
    picked = lax.dynamic_slice_in_dim(stats, head_turn * 2, 2, 2)
    return jnp.transpose(picked, (0, 2, 1))[..., None]


def place_stat(stats, values, head_turn):
    return lax.dynamic_update_slice_in_dim(
        stats, jnp.transpose(values[..., 0], (0, 2, 1)), head_turn * 2, 2
    )


def pair_scores(query_pair, key_pair, visible):
    scores = jnp.einsum(
        "gqhd,gkhd->ghqk", query_pair, key_pair, preferred_element_type=jnp.float32
    ) * HEAD ** (-0.5)
    return jnp.where(visible[None, None, :, :], scores, MASKED)


def attend_forward(queries, keys_all, values_all, visible):
    groups, row_count, width = queries.shape

    def head_body(head_turn, carried):
        attended, logsum = carried
        masked = pair_scores(head_pair(queries, head_turn), head_pair(keys_all, head_turn), visible)
        largest = jnp.max(masked, axis=-1, keepdims=True)
        powered = jnp.exp(masked - largest)
        totals = jnp.sum(powered, axis=-1, keepdims=True)
        shares = (powered / totals).astype(jnp.bfloat16)
        mixture = jnp.einsum(
            "ghqk,gkhd->gqhd",
            shares,
            head_pair(values_all, head_turn),
            preferred_element_type=jnp.float32,
        )
        attended = place_pair(attended, mixture, head_turn)
        logsum = place_stat(logsum, largest + jnp.log(totals), head_turn)
        return (attended, logsum)

    initial = (
        jnp.zeros((groups, row_count, width), jnp.float32),
        jnp.zeros((groups, row_count, width // HEAD), jnp.float32),
    )
    return lax.fori_loop(0, width // (2 * HEAD), head_body, initial)


def attend_backward(queries, keys_all, values_all, grad_attended, logsum, visible):
    groups, row_count, width = queries.shape
    key_count = keys_all.shape[1]

    def head_body(head_turn, carried):
        query_pair = head_pair(queries, head_turn)
        key_pair = head_pair(keys_all, head_turn)
        grad_pair = head_pair(grad_attended, head_turn)
        masked = pair_scores(query_pair, key_pair, visible)
        shares = jnp.exp(masked - stat_pair(logsum, head_turn))
        grad_shares = jnp.einsum(
            "gqhd,gkhd->ghqk",
            grad_pair,
            head_pair(values_all, head_turn),
            preferred_element_type=jnp.float32,
        )
        row_inner = jnp.sum(shares * grad_shares, axis=-1, keepdims=True)
        grad_scores = (shares * (grad_shares - row_inner)).astype(jnp.bfloat16)
        query_part = jnp.einsum(
            "ghqk,gkhd->gqhd", grad_scores, key_pair, preferred_element_type=jnp.float32
        ) * HEAD ** (-0.5)
        updated = (
            place_pair(carried[0], query_part, head_turn),
            place_stat(carried[1], row_inner, head_turn),
        )
        key_part = jnp.einsum(
            "ghqk,gqhd->gkhd", grad_scores, query_pair, preferred_element_type=jnp.float32
        ) * HEAD ** (-0.5)
        value_part = jnp.einsum(
            "ghqk,gqhd->gkhd",
            shares.astype(jnp.bfloat16),
            grad_pair,
            preferred_element_type=jnp.float32,
        )
        updated = updated + (
            place_pair(carried[2], key_part, head_turn),
            place_pair(carried[3], value_part, head_turn),
        )
        return updated

    initial = (
        jnp.zeros((groups, row_count, width), jnp.float32),
        jnp.zeros((groups, row_count, width // HEAD), jnp.float32),
    )
    initial = initial + (
        jnp.zeros((groups, key_count, width), jnp.float32),
        jnp.zeros((groups, key_count, width), jnp.float32),
    )
    return lax.fori_loop(0, width // (2 * HEAD), head_body, initial)


def vector_params(gathered):
    return tuple((member.astype(jnp.float32) for member in gathered[6:]))


def per_device(
    tokens,
    cotangent,
    w_query,
    w_key,
    w_value,
    w_output,
    w_inner,
    w_outer,
    bias_query,
    bias_value,
    bias_output,
    bias_inner,
    bias_outer,
    gain_input,
    bias_input,
    gain_attend,
    bias_attend,
    gain_middle,
    bias_middle,
    gain_hidden,
    bias_hidden,
):
    gathered = (
        lax.all_gather(w_query, ("dp", "seq"), axis=0, tiled=True),
        lax.all_gather(w_key, ("dp", "seq"), axis=0, tiled=True),
        lax.all_gather(w_value, ("dp", "seq"), axis=0, tiled=True),
        lax.all_gather(w_output, ("dp", "seq"), axis=0, tiled=True),
        lax.all_gather(w_inner, ("dp", "seq"), axis=0, tiled=True),
        lax.all_gather(w_outer, ("dp", "seq"), axis=0, tiled=True),
        lax.all_gather(bias_query, ("dp", "seq"), axis=0, tiled=True),
        lax.all_gather(bias_value, ("dp", "seq"), axis=0, tiled=True),
        lax.all_gather(bias_output, ("dp", "seq"), axis=0, tiled=True),
        lax.all_gather(bias_inner, ("dp", "seq"), axis=0, tiled=True),
        lax.all_gather(bias_outer, ("dp", "seq"), axis=0, tiled=True),
        lax.all_gather(gain_input, ("dp", "seq"), axis=0, tiled=True),
        lax.all_gather(bias_input, ("dp", "seq"), axis=0, tiled=True),
        lax.all_gather(gain_attend, ("dp", "seq"), axis=0, tiled=True),
        lax.all_gather(bias_attend, ("dp", "seq"), axis=0, tiled=True),
        lax.all_gather(gain_middle, ("dp", "seq"), axis=0, tiled=True),
        lax.all_gather(bias_middle, ("dp", "seq"), axis=0, tiled=True),
        lax.all_gather(gain_hidden, ("dp", "seq"), axis=0, tiled=True),
        lax.all_gather(bias_hidden, ("dp", "seq"), axis=0, tiled=True),
    )
    query_full, key_full, value_full, output_full, inner_full, outer_full = gathered[:6]
    (
        bq_full,
        bv_full,
        bo_full,
        bi_full,
        bu_full,
        gin_full,
        bin_full,
        gat_full,
        bat_full,
        gmi_full,
        bmi_full,
        ghi_full,
        bhi_full,
    ) = vector_params(gathered)
    groups, row_count, width = tokens.shape
    flat_rows = groups * row_count
    seq_place = lax.axis_index("seq")
    own_pos = seq_place * row_count + jnp.arange(row_count, dtype=jnp.int32)
    all_pos = jnp.arange(row_count * lax.axis_size("seq"), dtype=jnp.int32)
    visible = all_pos[None, :] // BLOCK <= own_pos[:, None] // BLOCK
    inputs = tokens.astype(jnp.float32).reshape(flat_rows, width)
    normed_low = layer_norm(inputs, gin_full, bin_full).astype(jnp.bfloat16)
    queries = (
        (product(normed_low, query_full) + bq_full)
        .astype(jnp.bfloat16)
        .reshape(groups, row_count, width)
    )
    keys_own = product(normed_low, key_full).astype(jnp.bfloat16).reshape(groups, row_count, width)
    values_own = (
        (product(normed_low, value_full) + bv_full)
        .astype(jnp.bfloat16)
        .reshape(groups, row_count, width)
    )
    keys_all, values_all = (
        lax.all_gather(keys_own, "seq", axis=1, tiled=True),
        lax.all_gather(values_own, "seq", axis=1, tiled=True),
    )
    attended, logsum = attend_forward(queries, keys_all, values_all, visible)
    attended = attended.reshape(flat_rows, width)
    sub_low = layer_norm(attended, gat_full, bat_full).astype(jnp.bfloat16)
    middle = inputs + product(sub_low, output_full) + bo_full
    normed_mid = layer_norm(middle, gmi_full, bmi_full).astype(jnp.bfloat16)
    hidden_pre = product(normed_mid, inner_full) + bi_full
    hidden_low = hidden_norm(hidden_pre, ghi_full, bhi_full).astype(jnp.bfloat16)
    output = (middle + product(hidden_low, outer_full) + bu_full).astype(jnp.bfloat16)
    regathered = (
        lax.all_gather(w_query, ("dp", "seq"), axis=0, tiled=True),
        lax.all_gather(w_key, ("dp", "seq"), axis=0, tiled=True),
        lax.all_gather(w_value, ("dp", "seq"), axis=0, tiled=True),
        lax.all_gather(w_output, ("dp", "seq"), axis=0, tiled=True),
        lax.all_gather(w_inner, ("dp", "seq"), axis=0, tiled=True),
        lax.all_gather(w_outer, ("dp", "seq"), axis=0, tiled=True),
        lax.all_gather(bias_query, ("dp", "seq"), axis=0, tiled=True),
        lax.all_gather(bias_value, ("dp", "seq"), axis=0, tiled=True),
        lax.all_gather(bias_output, ("dp", "seq"), axis=0, tiled=True),
        lax.all_gather(bias_inner, ("dp", "seq"), axis=0, tiled=True),
        lax.all_gather(bias_outer, ("dp", "seq"), axis=0, tiled=True),
        lax.all_gather(gain_input, ("dp", "seq"), axis=0, tiled=True),
        lax.all_gather(bias_input, ("dp", "seq"), axis=0, tiled=True),
        lax.all_gather(gain_attend, ("dp", "seq"), axis=0, tiled=True),
        lax.all_gather(bias_attend, ("dp", "seq"), axis=0, tiled=True),
        lax.all_gather(gain_middle, ("dp", "seq"), axis=0, tiled=True),
        lax.all_gather(bias_middle, ("dp", "seq"), axis=0, tiled=True),
        lax.all_gather(gain_hidden, ("dp", "seq"), axis=0, tiled=True),
        lax.all_gather(bias_hidden, ("dp", "seq"), axis=0, tiled=True),
    )
    keys_back, values_back = (
        lax.all_gather(keys_own, "seq", axis=1, tiled=True),
        lax.all_gather(values_own, "seq", axis=1, tiled=True),
    )
    query_back, key_back, value_back, output_back, inner_back, outer_back = regathered[:6]
    (
        bq_back,
        bv_back,
        bo_back,
        bi_back,
        bu_back,
        gin_back,
        bin_back,
        gat_back,
        bat_back,
        gmi_back,
        bmi_back,
        ghi_back,
        bhi_back,
    ) = vector_params(regathered)
    cotangent_flat = cotangent.reshape(flat_rows, width)
    grad_output = cotangent_flat.astype(jnp.float32)
    grad_w_outer = product_left(hidden_low, cotangent_flat)
    grad_bias_outer = column_sums(cotangent_flat)
    grad_hidden = product_right(cotangent_flat, outer_back)
    unused, pull_hidden = jax.vjp(hidden_norm, hidden_pre, ghi_back, bhi_back)
    grad_pre, grad_gain_hidden, grad_bias_hidden = pull_hidden(grad_hidden)
    grad_pre_low = grad_pre.astype(jnp.bfloat16)
    grad_w_inner = product_left(normed_mid, grad_pre_low)
    grad_bias_inner = column_sums(grad_pre_low)
    grad_normed_mid = product_right(grad_pre_low, inner_back)
    unused, pull_middle = jax.vjp(layer_norm, middle, gmi_back, bmi_back)
    grad_mid_part, grad_gain_middle, grad_bias_middle = pull_middle(grad_normed_mid)
    grad_middle = grad_output + grad_mid_part
    grad_branch = grad_middle.astype(jnp.bfloat16)
    grad_w_output = product_left(sub_low, grad_branch)
    grad_bias_output = column_sums(grad_branch)
    grad_sub = product_right(grad_branch, output_back)
    unused, pull_attend = jax.vjp(layer_norm, attended, gat_back, bat_back)
    grad_att, grad_gain_attend, grad_bias_attend = pull_attend(grad_sub)
    grad_attended = grad_att.astype(jnp.bfloat16).reshape(groups, row_count, width)
    grad_query, row_inner, key_part, value_part = attend_backward(
        queries, keys_back, values_back, grad_attended, logsum, visible
    )
    key_sum, value_sum = (
        lax.psum_scatter(
            key_part.astype(jnp.bfloat16), "seq", scatter_dimension=1, tiled=True
        ).astype(jnp.float32),
        lax.psum_scatter(
            value_part.astype(jnp.bfloat16), "seq", scatter_dimension=1, tiled=True
        ).astype(jnp.float32),
    )
    grad_query_low = grad_query.astype(jnp.bfloat16).reshape(flat_rows, width)
    grad_key_low = key_sum.astype(jnp.bfloat16).reshape(flat_rows, width)
    grad_value_low = value_sum.astype(jnp.bfloat16).reshape(flat_rows, width)
    grad_w_query = product_left(normed_low, grad_query_low)
    grad_bias_query = column_sums(grad_query_low)
    grad_w_key = product_left(normed_low, grad_key_low)
    grad_w_value = product_left(normed_low, grad_value_low)
    grad_bias_value = column_sums(grad_value_low)
    grad_normed = (
        product_right(grad_query_low, query_back)
        + product_right(grad_key_low, key_back)
        + product_right(grad_value_low, value_back)
    )
    unused, pull_input = jax.vjp(layer_norm, inputs, gin_back, bin_back)
    grad_in_part, grad_gain_input, grad_bias_input = pull_input(grad_normed)
    grad_tokens = (grad_middle + grad_in_part).reshape(groups, row_count, width)
    owned = (
        lax.psum_scatter(grad_w_query, ("dp", "seq"), scatter_dimension=0, tiled=True),
        lax.psum_scatter(grad_w_key, ("dp", "seq"), scatter_dimension=0, tiled=True),
        lax.psum_scatter(grad_w_value, ("dp", "seq"), scatter_dimension=0, tiled=True),
        lax.psum_scatter(grad_w_output, ("dp", "seq"), scatter_dimension=0, tiled=True),
        lax.psum_scatter(grad_w_inner, ("dp", "seq"), scatter_dimension=0, tiled=True),
        lax.psum_scatter(grad_w_outer, ("dp", "seq"), scatter_dimension=0, tiled=True),
        lax.psum_scatter(grad_bias_query, ("dp", "seq"), scatter_dimension=0, tiled=True),
        lax.psum_scatter(grad_bias_value, ("dp", "seq"), scatter_dimension=0, tiled=True),
        lax.psum_scatter(grad_bias_output, ("dp", "seq"), scatter_dimension=0, tiled=True),
        lax.psum_scatter(grad_bias_inner, ("dp", "seq"), scatter_dimension=0, tiled=True),
        lax.psum_scatter(grad_bias_outer, ("dp", "seq"), scatter_dimension=0, tiled=True),
        lax.psum_scatter(grad_gain_input, ("dp", "seq"), scatter_dimension=0, tiled=True),
        lax.psum_scatter(grad_bias_input, ("dp", "seq"), scatter_dimension=0, tiled=True),
        lax.psum_scatter(grad_gain_attend, ("dp", "seq"), scatter_dimension=0, tiled=True),
        lax.psum_scatter(grad_bias_attend, ("dp", "seq"), scatter_dimension=0, tiled=True),
        lax.psum_scatter(grad_gain_middle, ("dp", "seq"), scatter_dimension=0, tiled=True),
        lax.psum_scatter(grad_bias_middle, ("dp", "seq"), scatter_dimension=0, tiled=True),
        lax.psum_scatter(grad_gain_hidden, ("dp", "seq"), scatter_dimension=0, tiled=True),
        lax.psum_scatter(grad_bias_hidden, ("dp", "seq"), scatter_dimension=0, tiled=True),
    )
    return (
        output.reshape(groups, row_count, width),
        grad_tokens,
        owned[0],
        owned[1],
        owned[2],
        owned[3],
        owned[4],
        owned[5],
        owned[6],
        owned[7],
        owned[8],
        owned[9],
        owned[10],
        owned[11],
        owned[12],
        owned[13],
        owned[14],
        owned[15],
        owned[16],
        owned[17],
        owned[18],
    )


TILE = 256


def attend_kernel(query_ref, key_ref, value_ref, out_ref, log_ref, mask_s, top_s, sum_s, acc_s):
    heads = log_ref.shape[0]
    turn = pl.program_id(0)
    mask_s[...] = jnp.zeros(mask_s.shape, mask_s.dtype)
    for h in range(heads):
        mask_s[h, h * HEAD : (h + 1) * HEAD, :] = query_ref[h * HEAD : (h + 1) * HEAD, :]
    top_s[...] = jnp.full(top_s.shape, MASKED, jnp.float32)
    sum_s[...] = jnp.zeros(sum_s.shape, jnp.float32)
    acc_s[...] = jnp.zeros(acc_s.shape, jnp.float32)

    def step(j, carried):
        start = pl.multiple_of(j * TILE, TILE)
        keys = key_ref[pl.ds(start, TILE), :]
        for h in range(heads):
            rows = slice(h * HEAD, (h + 1) * HEAD)
            scores = jnp.dot(keys, mask_s[h], preferred_element_type=jnp.float32)
            top_old = top_s[h : h + 1, :]
            top_new = jnp.maximum(top_old, jnp.max(scores, axis=0, keepdims=True))
            powered = jnp.exp(scores - top_new)
            fade = jnp.exp(top_old - top_new)
            sum_s[h : h + 1, :] = sum_s[h : h + 1, :] * fade + jnp.sum(powered, axis=0, keepdims=True)
            top_s[h : h + 1, :] = top_new
            acc_s[rows, :] = acc_s[rows, :] * fade + jnp.dot(
                value_ref[rows, pl.ds(start, TILE)],
                powered.astype(jnp.bfloat16),
                preferred_element_type=jnp.float32,
            )
        return carried

    lax.fori_loop(0, turn + 1, step, 0)
    for h in range(heads):
        rows = slice(h * HEAD, (h + 1) * HEAD)
        total = sum_s[h : h + 1, :]
        out_ref[0, rows, :] = (acc_s[rows, :] / total).astype(out_ref.dtype)
        log_ref[h : h + 1, :] = top_s[h : h + 1, :] + jnp.log(total)


def attend_fast(flat, turned, heads, row_count):
    length = flat.shape[0]
    wide = turned.shape[0] // 3
    per_chunk = row_count // TILE
    return pl.pallas_call(
        attend_kernel,
        grid=(length // TILE,),
        in_specs=[
            pl.BlockSpec((wide, TILE), lambda i: (0, i)),
            pl.BlockSpec((length, wide), lambda i: (0, 1)),
            pl.BlockSpec((wide, length), lambda i: (2, 0)),
        ],
        out_specs=[
            pl.BlockSpec((1, heads * HEAD, TILE), lambda i: (i // per_chunk, 0, i % per_chunk)),
            pl.BlockSpec((heads, TILE), lambda i: (0, i)),
        ],
        out_shape=[
            jax.ShapeDtypeStruct((length // row_count, heads * HEAD, row_count), jnp.bfloat16),
            jax.ShapeDtypeStruct((heads, length), jnp.float32),
        ],
        scratch_shapes=[
            pltpu.VMEM((heads, wide, TILE), jnp.bfloat16),
            pltpu.VMEM((8, TILE), jnp.float32),
            pltpu.VMEM((8, TILE), jnp.float32),
            pltpu.VMEM((heads * HEAD, TILE), jnp.float32),
        ],
        name="attend_forward",
    )(turned, flat, turned)


def attend_back_kernel(
    query_ref, keyt_ref, queryn_ref, key_ref, value_ref, gradt_ref, grad_ref, log_ref, inner_ref,
    out_ref, qm_s, gm_s, qn_s, gn_s, dq_s, dk_s, dv_s,
):
    heads = log_ref.shape[0]
    wide = key_ref.shape[1]
    turn = pl.program_id(0)

    @pl.when(turn == 0)
    def _():
        dk_s[...] = jnp.zeros(dk_s.shape, jnp.float32)
        dv_s[...] = jnp.zeros(dv_s.shape, jnp.float32)

    qm_s[...] = jnp.zeros(qm_s.shape, qm_s.dtype)
    gm_s[...] = jnp.zeros(gm_s.shape, gm_s.dtype)
    dq_s[...] = jnp.zeros(dq_s.shape, jnp.float32)
    lane = lax.broadcasted_iota(jnp.int32, (TILE, wide), 1) // HEAD
    for h in range(heads):
        rows = slice(h * HEAD, (h + 1) * HEAD)
        qm_s[h, rows, :] = query_ref[rows, :]
        gm_s[h, rows, :] = gradt_ref[0, rows, :]
        qn_s[h] = jnp.where(lane == h, queryn_ref[...].astype(jnp.float32), 0.0).astype(jnp.bfloat16)
        gn_s[h] = jnp.where(lane == h, grad_ref[...].astype(jnp.float32), 0.0).astype(jnp.bfloat16)

    def step(j, carried):
        start = pl.multiple_of(j * TILE, TILE)
        keys = key_ref[pl.ds(start, TILE), :]
        values = value_ref[pl.ds(start, TILE), :]
        dk = dk_s[pl.ds(start, TILE), :]
        dv = dv_s[pl.ds(start, TILE), :]
        for h in range(heads):
            rows = slice(h * HEAD, (h + 1) * HEAD)
            scores = jnp.dot(keys, qm_s[h], preferred_element_type=jnp.float32)
            shares = jnp.exp(scores - log_ref[h : h + 1, :])
            grad_shares = jnp.dot(values, gm_s[h], preferred_element_type=jnp.float32)
            grad_scores = (shares * (grad_shares - inner_ref[h : h + 1, :])).astype(jnp.bfloat16)
            dv = dv + jnp.dot(shares.astype(jnp.bfloat16), gn_s[h], preferred_element_type=jnp.float32)
            dk = dk + jnp.dot(grad_scores, qn_s[h], preferred_element_type=jnp.float32)
            dq_s[rows, :] = dq_s[rows, :] + jnp.dot(
                keyt_ref[rows, pl.ds(start, TILE)], grad_scores, preferred_element_type=jnp.float32
            )
        dk_s[pl.ds(start, TILE), :] = dk
        dv_s[pl.ds(start, TILE), :] = dv
        return carried

    lax.fori_loop(0, turn + 1, step, 0)
    own = pl.multiple_of(turn * TILE, TILE)
    out_ref[pl.ds(own, TILE), 0:wide] = (jnp.transpose(dq_s[...]) * HEAD ** (-0.5)).astype(out_ref.dtype)

    @pl.when(turn == pl.num_programs(0) - 1)
    def _():
        out_ref[:, wide : 2 * wide] = dk_s[...].astype(out_ref.dtype)
        out_ref[:, 2 * wide : 3 * wide] = dv_s[...].astype(out_ref.dtype)


def attend_back_fast(flat, turned, gradt, grad, logsum, inner):
    length = flat.shape[0]
    heads = logsum.shape[0]
    wide = turned.shape[0] // 3
    row_count = gradt.shape[2]
    per_chunk = row_count // TILE
    return pl.pallas_call(
        attend_back_kernel,
        grid=(length // TILE,),
        in_specs=[
            pl.BlockSpec((wide, TILE), lambda i: (0, i)),
            pl.BlockSpec((wide, length), lambda i: (1, 0)),
            pl.BlockSpec((TILE, wide), lambda i: (i, 0)),
            pl.BlockSpec((length, wide), lambda i: (0, 1)),
            pl.BlockSpec((length, wide), lambda i: (0, 2)),
            pl.BlockSpec((1, heads * HEAD, TILE), lambda i: (i // per_chunk, 0, i % per_chunk)),
            pl.BlockSpec((TILE, wide), lambda i: (i, 0)),
            pl.BlockSpec((heads, TILE), lambda i: (0, i)),
            pl.BlockSpec((heads, TILE), lambda i: (0, i)),
        ],
        out_specs=pl.BlockSpec((length, 3 * wide), lambda i: (0, 0)),
        out_shape=jax.ShapeDtypeStruct((length, 3 * wide), jnp.bfloat16),
        scratch_shapes=[
            pltpu.VMEM((heads, wide, TILE), jnp.bfloat16),
            pltpu.VMEM((heads, wide, TILE), jnp.bfloat16),
            pltpu.VMEM((heads, TILE, wide), jnp.bfloat16),
            pltpu.VMEM((heads, TILE, wide), jnp.bfloat16),
            pltpu.VMEM((wide, TILE), jnp.float32),
            pltpu.VMEM((length, wide), jnp.float32),
            pltpu.VMEM((length, wide), jnp.float32),
        ],
        name="attend_backward",
    )(turned, turned, flat, flat, flat, gradt, grad, logsum, inner)


def swap_bit(part, axes, size, mask):
    return lax.ppermute(part, axes, [(i, i ^ mask) for i in range(size)])


def double_up(part, axes, size, order):
    bits = size.bit_length() - 1
    place = lax.axis_index(axes)
    shape = part.shape
    whole = part.reshape((1,) * bits + shape)
    for bit in order:
        upper = (place >> bit) & 1 == 1
        other = swap_bit(whole, axes, size, 1 << bit)
        whole = jnp.concatenate(
            [jnp.where(upper, other, whole), jnp.where(upper, whole, other)], axis=bits - 1 - bit
        )
    return whole.reshape((size,) + shape)


def halve_down(whole, axes, size, order, sent):
    bits = size.bit_length() - 1
    place = lax.axis_index(axes)
    shape = whole.shape[1:]
    part = whole.reshape((2,) * bits + shape)
    for bit in order:
        axis = bits - 1 - bit
        upper = (place >> bit) & 1 == 1
        low = lax.slice_in_dim(part, 0, 1, axis=axis)
        high = lax.slice_in_dim(part, 1, 2, axis=axis)
        away = jnp.where(upper, low, high).astype(sent)
        kept = jnp.where(upper, high, low).astype(jnp.float32)
        part = kept + swap_bit(away, axes, size, 1 << bit).astype(jnp.float32)
    return part.reshape(shape)


def line_gather(own, axes, size):
    place = lax.axis_index(axes)
    rows = own.shape[0]
    ups = []
    downs = []
    up = own
    down = own
    for far in range(1, size):
        up = lax.ppermute(up, axes, [(i, i + 1) for i in range(far - 1, size - 1)])
        down = lax.ppermute(down, axes, [(i, i - 1) for i in range(1, size - far + 1)])
        ups.append(up)
        downs.append(down)
    whole = jnp.zeros((size * rows,) + own.shape[1:], own.dtype)

    def put(whole, part, index):
        return lax.dynamic_update_slice_in_dim(whole, part, index * rows, 0)

    for far in range(size - 1, 0, -1):
        whole = put(whole, ups[far - 1], jnp.maximum(place - far, 0))
        whole = put(whole, downs[far - 1], jnp.minimum(place + far, size - 1))
    return put(whole, own, place)


def per_device_fast(
    dp_size,
    seq_size,
    tokens,
    cotangent,
    w_query,
    w_key,
    w_value,
    w_output,
    w_inner,
    w_outer,
    *vectors,
):
    both = ("dp", "seq")
    size = dp_size * seq_size
    bits = dp_size.bit_length() - 1
    seq_bits = seq_size.bit_length() - 1
    groups, row_count, width = tokens.shape
    hidden = w_inner.shape[1]
    own_rows = w_query.shape[0]
    inner_parts = hidden // width
    head_width = width // seq_size
    heads = head_width // HEAD
    wide = -(-head_width // 256) * 256
    length = row_count * seq_size
    own_tokens = tokens.reshape(row_count, width)

    sequence_low = line_gather(own_tokens, "seq", seq_size)

    joint = jnp.stack([w_query, w_key, w_value], axis=1).reshape(own_rows, 3, seq_size, head_width)
    joint = jnp.pad(jnp.transpose(joint, (2, 0, 1, 3)), ((0, 0), (0, 0), (0, 0), (0, wide - head_width)))
    joint = joint.reshape(seq_size, own_rows, 3 * wide)
    joint = lax.all_to_all(joint, "seq", 0, 0, tiled=True).reshape(seq_size * own_rows, 3 * wide)
    order = tuple(range(bits - 1, -1, -1))
    joint = double_up(joint, "dp", dp_size, order).reshape(width, 3 * wide)

    lengths = [v.shape[0] for v in vectors]
    packed = jnp.concatenate(vectors).reshape(1, -1)
    order_all = tuple(range(seq_bits)) + tuple(range(bits + seq_bits - 1, seq_bits - 1, -1))
    packed = double_up(packed, both, size, order_all).reshape(size, -1)
    full = []
    offset = 0
    for count in lengths:
        full.append(packed[:, offset : offset + count].reshape(size * count).astype(jnp.float32))
        offset += count
    (
        bq_full,
        bv_full,
        bo_full,
        bi_full,
        bu_full,
        gin_full,
        bin_full,
        gat_full,
        bat_full,
        gmi_full,
        bmi_full,
        ghi_full,
        bhi_full,
    ) = full

    inner_shard = jnp.transpose(w_inner.reshape(own_rows, inner_parts, width), (1, 0, 2))
    inner_shard = inner_shard.reshape(inner_parts * own_rows, width)
    outer_rows = w_outer.shape[0]
    stacked = jnp.concatenate([w_output, w_outer, inner_shard], axis=0)
    stacked = lax.all_gather(stacked, both, axis=0, tiled=False)
    output_full = stacked[:, :own_rows].reshape(width, width)
    outer_full = stacked[:, own_rows : own_rows + outer_rows].reshape(hidden, width)
    inner_full = jnp.concatenate(
        [
            stacked[:, own_rows + outer_rows + c * own_rows : own_rows + outer_rows + (c + 1) * own_rows].reshape(
                width, width
            )
            for c in range(inner_parts)
        ],
        axis=1,
    )

    seq_place = lax.axis_index("seq")
    sequence = sequence_low.astype(jnp.float32)
    normed_low = layer_norm(sequence, gin_full, bin_full).astype(jnp.bfloat16)

    def own_columns(vector):
        part = lax.dynamic_slice_in_dim(vector, seq_place * head_width, head_width, 0)
        return jnp.pad(part, (0, wide - head_width))

    joint_bias = jnp.concatenate([own_columns(bq_full), jnp.zeros((wide,), jnp.float32), own_columns(bv_full)])
    joint_scale = jnp.concatenate(
        [jnp.full((wide,), HEAD ** (-0.5), jnp.float32), jnp.ones((2 * wide,), jnp.float32)]
    )
    flat = ((product(normed_low, joint) + joint_bias) * joint_scale).astype(jnp.bfloat16)
    turned = jnp.transpose(flat)
    mixed, logsum = attend_fast(flat, turned, heads, row_count)

    attended = lax.all_to_all(mixed, "seq", 0, 0, tiled=True).reshape(width, row_count)
    attended = jnp.transpose(attended).astype(jnp.float32)
    inputs = own_tokens.astype(jnp.float32)
    sub_low = layer_norm(attended, gat_full, bat_full).astype(jnp.bfloat16)
    middle = inputs + product(sub_low, output_full) + bo_full
    normed_mid = layer_norm(middle, gmi_full, bmi_full).astype(jnp.bfloat16)
    hidden_pre = product(normed_mid, inner_full) + bi_full
    hidden_low = hidden_norm(hidden_pre, ghi_full, bhi_full).astype(jnp.bfloat16)
    output = (middle + product(hidden_low, outer_full) + bu_full).astype(jnp.bfloat16)

    cotangent_flat = cotangent.reshape(row_count, width)
    grad_output = cotangent_flat.astype(jnp.float32)
    grad_w_outer = product_left(hidden_low, cotangent_flat)
    grad_bias_outer = column_sums(cotangent_flat)
    grad_hidden = product_right(cotangent_flat, outer_full)
    unused, pull_hidden = jax.vjp(hidden_norm, hidden_pre, ghi_full, bhi_full)
    grad_pre, grad_gain_hidden, grad_bias_hidden = pull_hidden(grad_hidden)
    grad_pre_low = grad_pre.astype(jnp.bfloat16)
    grad_w_inner = product_left(normed_mid, grad_pre_low)
    grad_bias_inner = column_sums(grad_pre_low)
    grad_normed_mid = product_right(grad_pre_low, inner_full)
    unused, pull_middle = jax.vjp(layer_norm, middle, gmi_full, bmi_full)
    grad_mid_part, grad_gain_middle, grad_bias_middle = pull_middle(grad_normed_mid)
    grad_middle = grad_output + grad_mid_part
    grad_branch = grad_middle.astype(jnp.bfloat16)
    grad_w_output = product_left(sub_low, grad_branch)
    grad_bias_output = column_sums(grad_branch)
    grad_sub = product_right(grad_branch, output_full)
    unused, pull_attend = jax.vjp(layer_norm, attended, gat_full, bat_full)
    grad_att, grad_gain_attend, grad_bias_attend = pull_attend(grad_sub)

    big = jnp.concatenate(
        [
            grad_w_output.astype(jnp.bfloat16).reshape(size, own_rows, width),
            grad_w_outer.astype(jnp.bfloat16).reshape(size, outer_rows, width),
        ]
        + [
            grad_w_inner[:, c * width : (c + 1) * width].astype(jnp.bfloat16).reshape(size, own_rows, width)
            for c in range(inner_parts)
        ],
        axis=1,
    )
    big = lax.psum_scatter(big, both, scatter_dimension=0, tiled=False).astype(jnp.float32)
    owned_output = big[:own_rows]
    owned_outer = big[own_rows : own_rows + outer_rows]
    owned_inner = jnp.transpose(
        big[own_rows + outer_rows :].reshape(inner_parts, own_rows, width), (1, 0, 2)
    ).reshape(own_rows, hidden)

    gradt = jnp.transpose(grad_att.astype(jnp.bfloat16)).reshape(seq_size, head_width, row_count)
    gradt = lax.all_to_all(gradt, "seq", 0, 0, tiled=True)
    inner_sums = jnp.sum(
        (gradt.astype(jnp.float32) * mixed.astype(jnp.float32)).reshape(seq_size, heads, HEAD, row_count), axis=2
    )
    inner_sums = jnp.transpose(inner_sums, (1, 0, 2)).reshape(heads, length)
    grad_mixed = jnp.pad(
        jnp.transpose(gradt, (0, 2, 1)).reshape(length, head_width), ((0, 0), (0, wide - head_width))
    )
    joint_grad = attend_back_fast(flat, turned, gradt, grad_mixed, logsum, inner_sums)

    grad_normed_part = product_right(joint_grad, joint)
    mean = jnp.mean(sequence, axis=-1, keepdims=True)
    centered = sequence - mean
    scaled = centered * lax.rsqrt(jnp.mean(centered * centered, axis=-1, keepdims=True) + EPSILON)
    grad_gain_input = jnp.sum(grad_normed_part * scaled, axis=0)
    grad_bias_input = jnp.sum(grad_normed_part, axis=0)
    pieces = grad_normed_part.astype(jnp.bfloat16).reshape(seq_size, row_count, width)
    pieces = lax.all_to_all(pieces, "seq", 0, 0, tiled=True)
    grad_normed = jnp.sum(pieces.astype(jnp.float32), axis=0)

    joint_sums = column_sums(joint_grad)

    def spread(sums):
        return lax.dynamic_update_slice_in_dim(
            jnp.zeros((width,), jnp.float32), sums[:head_width], seq_place * head_width, 0
        )

    grad_bias_query = spread(joint_sums[:wide])
    grad_bias_value = spread(joint_sums[2 * wide :])

    joint_w = product_left(normed_low, joint_grad).reshape(dp_size, seq_size * own_rows, 3 * wide)
    joint_w = halve_down(joint_w, "dp", dp_size, tuple(range(bits)), jnp.bfloat16)
    joint_w = joint_w.astype(jnp.bfloat16).reshape(seq_size, own_rows, 3, wide)[..., :head_width]
    joint_w = lax.all_to_all(joint_w.reshape(seq_size, own_rows, 3 * head_width), "seq", 0, 0, tiled=True)
    joint_w = joint_w.astype(jnp.float32).reshape(seq_size, own_rows, 3, head_width)
    owned_joint = [jnp.transpose(joint_w[:, :, n], (1, 0, 2)).reshape(own_rows, width) for n in range(3)]

    grads = [
        grad_bias_query,
        grad_bias_value,
        grad_bias_output,
        grad_bias_inner,
        grad_bias_outer,
        grad_gain_input,
        grad_bias_input,
        grad_gain_attend,
        grad_bias_attend,
        grad_gain_middle,
        grad_bias_middle,
        grad_gain_hidden,
        grad_bias_hidden,
    ]
    packed_grads = jnp.concatenate([g.reshape(size, -1) for g in grads], axis=1)
    order_down = tuple(range(seq_bits, seq_bits + bits)) + tuple(range(seq_bits - 1, -1, -1))
    packed_grads = halve_down(packed_grads, both, size, order_down, jnp.float32)
    owned_vectors = []
    offset = 0
    for count in lengths:
        owned_vectors.append(packed_grads[offset : offset + count])
        offset += count

    unused, pull_input = jax.vjp(layer_norm, inputs, gin_full, bin_full)
    grad_in_part = pull_input(grad_normed)[0]
    grad_tokens = grad_middle + grad_in_part
    return (
        output.reshape(groups, row_count, width),
        grad_tokens.reshape(groups, row_count, width),
        *owned_joint,
        owned_output,
        owned_inner,
        owned_outer,
        *owned_vectors,
    )


def is_power(count):
    return count & (count - 1) == 0


def solution(mesh):
    dp_size = mesh.shape["dp"]
    seq_size = mesh.shape["seq"]
    row_spec = P("dp", "seq", None)
    matrix_spec = P(("dp", "seq"), None)
    vector_spec = P(("dp", "seq"))

    def choose(*arrays):
        groups, row_count, width = arrays[0].shape
        fits = groups == 1 and row_count % TILE == 0 and width % (seq_size * HEAD) == 0
        fits = fits and arrays[6].shape[1] % width == 0
        if fits and is_power(dp_size) and is_power(seq_size):
            return per_device_fast(dp_size, seq_size, *arrays)
        return per_device(*arrays)

    return jax.shard_map(
        choose,
        mesh=mesh,
        in_specs=(row_spec,) * 2 + (matrix_spec,) * 6 + (vector_spec,) * 13,
        out_specs=(row_spec,) * 2 + (matrix_spec,) * 6 + (vector_spec,) * 13,
        check_vma=False,
    )
```
